256 devices in a mesh: layer: 32 (over x, z), box: 8 (over y, core).
Axes of the slice: x: 4, y: 4, z: 8, core: 2. Of those that a mesh axis runs over, the one named last changes fastest.
Arguments:
- box_maps: bfloat16 [32, 8192, 1024], P('layer', 'box'), may hold values from -0.1875 to 0.1875
- block_pattern: int32 [32, 64, 8], P('layer', 'box'), may hold values 0 or 1
- face_inverses: float32 [32, 7, 256, 256], P('layer'), may hold values from -0.375 to 0.375
- index_map: int32 [32, 1024], P('layer'), may hold values from 0 to 1023, each once within a row
- sources: float32 [32, 16, 1024], P('layer', 'box'), may hold values from -2.5 to 2.5
Outputs:
- merged: bfloat16 [32, 1024, 1024], P('layer')
- sweep_trace: float32 [32, 16, 1024], P('layer', 'box')
The draws below stay inside these ranges and needn't reach their ends.
Inputs may be any that keep to these rules, and one draw needn't show every extreme that they name: Each row of index_map is a permutation of 0 to 1023.
All inputs are finite; a program needn't handle non-finite values. No bound on the sum of `block_pattern` on one device may be relied on, other than what follows from the above.
Results may differ from the reference program's by a relative error of at most 0.025.
Values may be sent and summed in bfloat16 or wider, within the bound.
A program may use at most 64 MiB of HBM per device.

```python
import math
import jax
import jax.numpy as jnp
from jax import lax

W = 1024
BLK = 128
K = 256
R = 16
WB = 8
LAYERS = 32
N_BOX = 8


def draw_box_maps(key, part):
    shape = (LAYERS, N_BOX * W, W)
    spread = 1.0 / math.sqrt(W)
    values = jnp.clip(jax.random.normal(key, shape, jnp.float32), -6.0, 6.0) * spread
    return values.astype(jnp.bfloat16)


def draw_face_inverses(key, part):
    shape = (LAYERS, N_BOX - 1, K, K)
    spread = 1.0 / math.sqrt(K)
    values = jnp.clip(jax.random.normal(key, shape, jnp.float32), -6.0, 6.0) * spread
    return values.astype(jnp.float32)


def touch_ends(entries, own_key, least, top_value):
    longest = entries.shape.index(max(entries.shape))
    spots = []
    for shift in (0, 1):
        where = [jax.random.randint(jax.random.fold_in(own_key, axis), (), 0, length) for axis, length in enumerate(entries.shape)]
        where[longest] = (where[longest] + shift) % entries.shape[longest]
        spots.append(tuple(where))
    return entries.at[spots[0]].set(least).at[spots[1]].set(top_value)


def shard_levels(key, extent, pieces, least, high):
    def one(position, parts):
        draws = jax.random.uniform(jax.random.fold_in(jax.random.fold_in(key, 6), position), (parts,), jnp.float32, least / len(pieces), high / len(pieces))
        return jnp.repeat(jnp.exp(draws), extent[position] // parts).reshape((-1,) + (1,) * (len(extent) - position - 1))

    gain = one(*pieces[0])
    for cut in pieces[1:]:
        gain = gain * one(*cut)
    return gain


def normal_values(rng, extent, scale, most, split=(), kind=jnp.bfloat16):
    loudness = shard_levels(rng, extent, split, -0.22, 0.18) if split else 1.0
    result = jax.random.normal(rng, extent, jnp.float32) * scale * loudness
    return jnp.minimum(jnp.maximum(result, -most), most).astype(kind)


def setup_inputs(seed: int = 0) -> dict:
    key_of = jax.random.split(jax.random.key(seed), 6)
    return {
        "box_maps": draw_box_maps(jax.random.fold_in(key_of[5], 71), 0),
        "block_pattern": touch_ends((jax.random.randint(key_of[1], (LAYERS, N_BOX * WB, WB), 0, 4) < 3).astype(jnp.int32), jax.random.fold_in(key_of[1], 1), 0, 1),
        "face_inverses": draw_face_inverses(jax.random.fold_in(key_of[5], 71), 0),
        "index_map": jax.vmap(lambda own: jax.random.permutation(own, W))(jax.random.split(key_of[3], LAYERS)).reshape((LAYERS, W)).astype(jnp.int32),
        "sources": normal_values(key_of[4], (LAYERS, R, W), 0.35, 2.5, ((0, 32), (1, 8)), jnp.float32),
    }


def mask_map(one_map, one_pattern):
    tiles = one_map.reshape(WB, BLK, WB, BLK)
    kept = one_pattern.astype(jnp.bfloat16)[:, None, :, None]
    return (tiles * kept).reshape(W, W)


def combine(first, second, inverse, level):
    joined = 0.5 * (first.astype(jnp.float32) + second.astype(jnp.float32))
    left_cols = joined[:, level * K:(level + 1) * K]
    right_rows = joined[level * K:(level + 1) * K, :]
    product = jnp.dot(left_cols, inverse, precision=lax.Precision.HIGHEST)
    return (joined - jnp.dot(product, right_rows, precision=lax.Precision.HIGHEST)).astype(jnp.bfloat16)


def merge_tree(maps_layer, pattern_layer, inverses_layer):
    tree_nodes = [mask_map(maps_layer[b * W:(b + 1) * W], pattern_layer[b * WB:(b + 1) * WB]) for b in range(N_BOX)]
    level = 0
    while len(tree_nodes) > 1:
        renewed = []
        for couple in range(len(tree_nodes) // 2):
            tree_node = (N_BOX >> (level + 1)) - 1 + couple
            renewed.append(combine(tree_nodes[2 * couple], tree_nodes[2 * couple + 1], inverses_layer[tree_node], level))
        tree_nodes = renewed
        level = level + 1
    return tree_nodes[0]


def reference(box_maps, block_pattern, face_inverses, index_map, sources):
    coupling = float(N_BOX) ** 0.5
    merged = lax.map(lambda t: merge_tree(t[0], t[1], t[2]), (box_maps, block_pattern, face_inverses))

    def down_step(previous, t):
        layer_map, order_map, source_rows = t
        gathered = previous[:, order_map].astype(jnp.bfloat16)
        current = source_rows + coupling * jnp.dot(gathered, layer_map.T, preferred_element_type=jnp.float32)
        return current, current

    initial = jnp.zeros((R, W), jnp.float32)
    _, downward = lax.scan(down_step, initial, (merged, index_map, sources))

    def up_step(following, t):
        layer_map, down_rows = t
        current = down_rows + coupling * jnp.dot(following.astype(jnp.bfloat16), layer_map, preferred_element_type=jnp.float32)
        return current, current

    _, upward = lax.scan(up_step, initial, (merged, downward), reverse=True)
    return merged, upward
```

```python
import jax
import jax.numpy as jnp
from jax import lax
from jax.experimental import pallas as pl
from jax.experimental.pallas import tpu as pltpu
from jax.sharding import PartitionSpec as P

MESH = pl.DeviceIdType.MESH
NT = (((1,), (1,)), ((), ()))


def partner_2(value, axis, distance):
    mask = 2**distance
    pairs = [(source, source ^ mask) for source in range(lax.axis_size(axis))]
    return lax.ppermute(value, axis, pairs)


def mask_map(one_map, one_pattern):
    blocks_count = one_pattern.shape[0]
    width = one_map.shape[0]
    tiles = one_map.reshape(
        blocks_count, width // blocks_count, blocks_count, width // blocks_count
    )
    kept = one_pattern.astype(jnp.bfloat16)[:, None, :, None]
    return (tiles * kept).reshape(width, width)


def combine(first, second, inverse, level):
    face_size = inverse.shape[0]
    joined = 0.5 * (first.astype(jnp.float32) + second.astype(jnp.float32))
    left_cols = joined[:, level * face_size : (level + 1) * face_size]
    right_rows = joined[level * face_size : (level + 1) * face_size, :]
    product = jnp.dot(left_cols, inverse, precision=lax.Precision.HIGHEST)
    return (joined - jnp.dot(product, right_rows, precision=lax.Precision.HIGHEST)).astype(
        jnp.bfloat16
    )


def sweep_kernel(layers, coupling, m_ref, idx_ref, src_ref, out_ref, a_ref, send_buf, down_buf, up_buf, sems):
    me = lax.axis_index("layer")
    box = lax.axis_index("box")
    width = m_ref.shape[0]

    barrier = pltpu.get_barrier_semaphore()

    for near in (lax.rem(me + 1, layers), lax.rem(me + layers - 1, layers)):
        pl.semaphore_signal(barrier, inc=1, device_id=(near, box), device_id_type=MESH)
    pl.semaphore_wait(barrier, 2)

    rows = 256

    @pl.loop(0, width // rows)
    def _(step):
        base = pl.multiple_of(step * rows, rows)
        spot = lax.broadcasted_iota(jnp.int32, (rows, width), 0) + base
        onehot = (spot == idx_ref[...]).astype(jnp.float32).astype(jnp.bfloat16)
        a_ref[pl.ds(base, rows), :] = lax.dot_general(
            onehot, m_ref[...], NT, preferred_element_type=jnp.float32
        ).astype(jnp.bfloat16)

    def to(buf, slot, where):
        return pltpu.make_async_remote_copy(
            src_ref=send_buf.at[slot],
            dst_ref=buf,
            send_sem=sems.at[slot],
            recv_sem=sems.at[2 + slot],
            device_id=(where, box),
            device_id_type=MESH,
        )

    down_copy = to(down_buf, 0, jnp.minimum(me + 1, layers - 1))
    up_copy = to(up_buf, 1, jnp.maximum(me - 1, 0))

    @pl.when(me == 0)
    def _():
        out_ref[...] = src_ref[...]

    @pl.when(me > 0)
    def _():
        down_copy.wait_recv()
        out_ref[...] = src_ref[...] + coupling * jnp.dot(
            down_buf[...], a_ref[...], preferred_element_type=jnp.float32
        )

    @pl.when(me < layers - 1)
    def _():
        send_buf[0] = out_ref[...].astype(jnp.bfloat16)
        down_copy.start()
        up_copy.wait_recv()
        out_ref[...] += coupling * jnp.dot(
            up_buf[...], m_ref[...], preferred_element_type=jnp.float32
        )

    @pl.when(me > 0)
    def _():
        send_buf[1] = out_ref[...].astype(jnp.bfloat16)
        up_copy.start()

    @pl.when(me < layers - 1)
    def _():
        down_copy.wait_send()

    @pl.when(me > 0)
    def _():
        up_copy.wait_send()


def on_device(box_maps, block_pattern, face_inverses, index_map, sources):
    boxes = lax.axis_size("box")
    layers = lax.axis_size("layer")
    coupling = float(boxes) ** 0.5
    levels = boxes.bit_length() - 1
    inverses = face_inverses[0]
    current = mask_map(box_maps[0], block_pattern[0])
    position = lax.axis_index("box")
    for level in range(levels):
        partner = partner_2(current, "box", level)
        tree_node = (boxes >> level + 1) - 1 + (position >> level + 1)
        chosen = lax.dynamic_index_in_dim(inverses, tree_node, 0, keepdims=False)
        current = combine(current, partner, chosen, level)
    merged = current
    width = merged.shape[0]
    rhs = sources.shape[1]
    import functools
    vmem = pl.BlockSpec(memory_space=pltpu.VMEM)
    upward = pl.pallas_call(
        functools.partial(sweep_kernel, layers, coupling),
        out_shape=jax.ShapeDtypeStruct((rhs, width), jnp.float32),
        in_specs=[vmem] * 3,
        out_specs=vmem,
        scratch_shapes=[
            pltpu.VMEM((width, width), jnp.bfloat16),
            pltpu.VMEM((2, rhs, width), jnp.bfloat16),
            pltpu.VMEM((rhs, width), jnp.bfloat16),
            pltpu.VMEM((rhs, width), jnp.bfloat16),
            pltpu.SemaphoreType.DMA((4,)),
        ],
        compiler_params=pltpu.CompilerParams(
            collective_id=0, has_side_effects=True, vmem_limit_bytes=48 * 2**20
        ),
    )(merged, index_map, sources[0])
    return (merged[None], upward[None])


def solution(mesh):
    return jax.shard_map(
        on_device,
        mesh=mesh,
        in_specs=(
            P("layer", "box", None),
            P("layer", "box", None),
            P("layer", None, None, None),
            P("layer", None),
            P("layer", "box", None),
        ),
        out_specs=(P("layer", None, None), P("layer", "box", None)),
        check_vma=False,
    )
```

```python
import functools
import math

import jax
import jax.numpy as jnp
from jax import lax
from jax.experimental import pallas as pl
from jax.experimental.pallas import tpu as pltpu
from jax.sharding import PartitionSpec as P

MESH = pl.DeviceIdType.MESH
NT = (((1,), (1,)), ((), ()))
F32 = jnp.float32
BF16 = jnp.bfloat16
CH = 128
ORDER = (2, 4, 0, 6)


def kernel(
    layers, coupling, map_ref, keep_ref, inv_ref, idx_ref, src_ref,
    m_ref, out_ref,
    leaf, part0, half1, part1, half2, part2, v_ref, pick, a_ref,
    send_buf, down_buf, up_buf,
    s0, r0, s1, r1, s2, r2, q1, q2, sems,
):
    me = lax.axis_index("layer")
    box = lax.axis_index("box")
    width = m_ref.shape[0]
    face = inv_ref.shape[1]
    core = lax.rem(box, 2)
    chip = box // 2
    sibling = box + 1 - 2 * core
    pair = 2 * (chip + 1 - 2 * lax.rem(chip, 2)) + core
    cross = 2 * (3 - chip) + core

    barrier = pltpu.get_barrier_semaphore()
    for near in (lax.rem(me + 1, layers), lax.rem(me + layers - 1, layers)):
        pl.semaphore_signal(barrier, inc=1, device_id=(near, box), device_id_type=MESH)
    for mate in (sibling, pair, cross):
        pl.semaphore_signal(barrier, inc=1, device_id=(me, mate), device_id_type=MESH)
    pl.semaphore_wait(barrier, 5)

    def rows(k):
        return pl.ds(pl.multiple_of(k * CH, CH), CH)

    def send(src, dst, k, ssem, rsem, mate):
        return pltpu.make_async_remote_copy(
            src_ref=src.at[rows(k), :], dst_ref=dst.at[rows(k), :],
            send_sem=ssem.at[k], recv_sem=rsem.at[k],
            device_id=(me, mate), device_id_type=MESH,
        )

    def joined(own, other, where):
        return 0.5 * (own[where, :].astype(F32) + other[where, :].astype(F32))

    def make_v(level, own, other):
        for part in range(face // CH):
            where = pl.ds(level * face + part * CH, CH)
            v_ref[level, pl.ds(part * CH, CH), :] = joined(own, other, where).astype(BF16)

    places = (3 + box // 2, 1 + box // 4, 0)

    def merge(level, own, other, out, k):
        whole = joined(own, other, rows(k))
        left = whole[:, level * face : (level + 1) * face].astype(BF16)
        inner = inv_ref[places[level]].astype(BF16)
        product = jnp.dot(left, inner, preferred_element_type=F32).astype(BF16)
        out[rows(k), :] = (
            whole - jnp.dot(product, v_ref[level], preferred_element_type=F32)
        ).astype(BF16)

    for k in range(width // CH):
        leaf[rows(k), :] = (map_ref[rows(k), :].astype(F32) * keep_ref[pl.ds(k, 1), :]).astype(BF16)
        send(leaf, part0, k, s0, r0, sibling).start()

    @pl.loop(0, width // CH)
    def _(step):
        spot = lax.broadcasted_iota(jnp.int32, (CH, width), 0) + step * CH
        pick[rows(step), :] = (spot == idx_ref[...]).astype(F32).astype(BF16)

    def got(buf, k, ssem, rsem, mate):
        send(buf, buf, k, ssem, rsem, mate).wait_recv()

    for k in range(2):
        got(part0, k, s0, r0, sibling)
    make_v(0, leaf, part0)
    for k in range(2, width // CH):
        got(part0, k, s0, r0, sibling)
    for base in ORDER:
        mine, theirs = base + core, base + 1 - core
        merge(0, leaf, part0, half1, mine)
        send(half1, part1, mine, s1, r1, pair).start()
        merge(0, leaf, part0, half1, theirs)

    def permute(k):
        a_ref[:, rows(k)] = lax.dot_general(
            pick[...], m_ref[rows(k), :], NT, preferred_element_type=F32
        ).astype(BF16)

    def last(step):
        mine, theirs = ORDER[step] + core, ORDER[step] + 1 - core
        got(part2, mine, s2, r2, cross)
        send(part2, part2, mine, q2, r2, sibling).start()
        got(part2, theirs, q2, r2, sibling)
        if step == 0:
            return
        if step == 1:
            make_v(2, half2, part2)
        for other in (0, 1) if step == 1 else (step,):
            for k in (ORDER[other], ORDER[other] + 1):
                merge(2, half2, part2, m_ref, k)
                permute(k)

    for step, base in enumerate(ORDER):
        mine, theirs = base + core, base + 1 - core
        got(part1, mine, s1, r1, pair)
        send(part1, part1, mine, q1, r1, sibling).start()
        if step == 0:
            got(part1, theirs, q1, r1, sibling)
            make_v(1, half1, part1)
        merge(1, half1, part1, half2, mine)
        send(half2, part2, mine, s2, r2, cross).start()
        if step > 0:
            got(part1, theirs, q1, r1, sibling)
        merge(1, half1, part1, half2, theirs)
        if step > 0:
            last(step - 1)
    last(len(ORDER) - 1)

    def to(buf, slot, where):
        return pltpu.make_async_remote_copy(
            src_ref=send_buf.at[slot],
            dst_ref=buf,
            send_sem=sems.at[slot],
            recv_sem=sems.at[2 + slot],
            device_id=(where, box),
            device_id_type=MESH,
        )

    down_copy = to(down_buf, 0, jnp.minimum(me + 1, layers - 1))
    up_copy = to(up_buf, 1, jnp.maximum(me - 1, 0))

    @pl.when(me == 0)
    def _():
        out_ref[...] = src_ref[...]

    @pl.when(me > 0)
    def _():
        down_copy.wait_recv()
        out_ref[...] = src_ref[...] + coupling * jnp.dot(
            down_buf[...], a_ref[...], preferred_element_type=jnp.float32
        )

    @pl.when(me < layers - 1)
    def _():
        send_buf[0] = out_ref[...].astype(jnp.bfloat16)
        down_copy.start()
        up_copy.wait_recv()
        out_ref[...] += coupling * jnp.dot(
            up_buf[...], m_ref[...], preferred_element_type=jnp.float32
        )

    @pl.when(me > 0)
    def _():
        send_buf[1] = out_ref[...].astype(jnp.bfloat16)
        up_copy.start()

    @pl.when(me < layers - 1)
    def _():
        down_copy.wait_send()

    @pl.when(me > 0)
    def _():
        up_copy.wait_send()

    for k in range(width // CH):
        send(leaf, part0, k, s0, r0, sibling).wait_send()
    for base in ORDER:
        mine = base + core
        send(half1, part1, mine, s1, r1, pair).wait_send()
        send(half2, part2, mine, s2, r2, cross).wait_send()
        send(part1, part1, mine, q1, r1, sibling).wait_send()
        send(part2, part2, mine, q2, r2, sibling).wait_send()


def on_device(box_maps, block_pattern, face_inverses, index_map, sources):
    boxes = lax.axis_size("box")
    layers = lax.axis_size("layer")
    coupling = math.sqrt(boxes)
    width = box_maps.shape[2]
    rhs = sources.shape[1]
    face = face_inverses.shape[2]
    keep = jnp.repeat(block_pattern[0].astype(F32), width // block_pattern.shape[2], axis=1)
    vmem = pl.BlockSpec(memory_space=pltpu.VMEM)
    square = pltpu.VMEM((width, width), BF16)
    count = pltpu.SemaphoreType.DMA((width // CH,))
    merged, upward = pl.pallas_call(
        functools.partial(kernel, layers, coupling),
        out_shape=(
            jax.ShapeDtypeStruct((width, width), BF16),
            jax.ShapeDtypeStruct((rhs, width), F32),
        ),
        in_specs=[vmem] * 5,
        out_specs=(vmem, vmem),
        scratch_shapes=[square] * 6
        + [pltpu.VMEM((3, face, width), BF16), square, square]
        + [
            pltpu.VMEM((2, rhs, width), BF16),
            pltpu.VMEM((rhs, width), BF16),
            pltpu.VMEM((rhs, width), BF16),
        ]
        + [count] * 8
        + [pltpu.SemaphoreType.DMA((4,))],
        compiler_params=pltpu.CompilerParams(
            collective_id=0, has_side_effects=True, vmem_limit_bytes=56 * 2**20
        ),
    )(box_maps[0], keep, face_inverses[0], index_map, sources[0])
    return (merged[None], upward[None])


def solution(mesh):
    return jax.shard_map(
        on_device,
        mesh=mesh,
        in_specs=(
            P("layer", "box", None),
            P("layer", "box", None),
            P("layer", None, None, None),
            P("layer", None),
            P("layer", "box", None),
        ),
        out_specs=(P("layer", None, None), P("layer", "box", None)),
        check_vma=False,
    )
```

```python
import functools
import math

import jax
import jax.numpy as jnp
from jax import lax
from jax.experimental import pallas as pl
from jax.experimental.pallas import tpu as pltpu
from jax.sharding import PartitionSpec as P

MESH = pl.DeviceIdType.MESH
NT = (((1,), (1,)), ((), ()))
F32 = jnp.float32
BF16 = jnp.bfloat16
CH = 128
ORDER = (2, 4, 0, 6)


def kernel(
    layers, coupling, map_ref, keep_ref, inv_ref, idx_ref, src_ref,
    m_ref, out_ref,
    leaf, part0, half1, part1, half2, part2, v_ref, pick, a_ref,
    d_ref, u_ref, send_d, send_u, down_buf, up_buf,
    phi, phi_in, psi, psi_in, res, res_in,
    dcol, ucol, flat, part3, link_d, link_u, in_d, in_u, col16, last_in,
    s0, r0, s1, r1, s2, r2, q1, q2,
    phi_s, phi_r, psi_s, psi_r, res_s, res_r, one_s, one_r,
    ld_s, ld_r, lu_s, lu_r, bd_s, bu_s, f_s, f_r,
):
    me = lax.axis_index("layer")
    box = lax.axis_index("box")
    width = m_ref.shape[0]
    face = inv_ref.shape[1]
    core = lax.rem(box, 2)
    chip = box // 2
    sibling = box + 1 - 2 * core
    pair = 2 * (chip + 1 - 2 * lax.rem(chip, 2)) + core
    cross = 2 * (3 - chip) + core

    depth = 8
    blocks = layers // depth
    boxes = 8
    group = me // depth
    z = lax.rem(me, depth)
    first, final = z == 0, z == depth - 1
    top, bottom = group == 0, group == blocks - 1

    barrier = pltpu.get_barrier_semaphore()

    def greet(layer, mate):
        pl.semaphore_signal(barrier, inc=1, device_id=(layer, mate), device_id_type=MESH)

    for step in range(1, boxes):
        greet(me, lax.rem(box + step, boxes))
    for step in range(1, depth):
        greet(group * depth + lax.rem(z + step, depth), box)
    for step in (1, blocks - 1):
        for mate in range(boxes):
            greet(lax.rem(group + step, blocks) * depth + z, mate)
    for k in range(width // CH):
        leaf[pl.ds(k * CH, CH), :] = (
            map_ref[pl.ds(k * CH, CH), :].astype(F32) * keep_ref[pl.ds(k, 1), :]
        ).astype(BF16)
    pl.semaphore_wait(barrier, boxes - 1 + depth - 1 + 2 * boxes)

    def rows(k):
        return pl.ds(pl.multiple_of(k * CH, CH), CH)

    def send(src, dst, k, ssem, rsem, mate):
        return pltpu.make_async_remote_copy(
            src_ref=src.at[rows(k), :], dst_ref=dst.at[rows(k), :],
            send_sem=ssem.at[k], recv_sem=rsem.at[k],
            device_id=(me, mate), device_id_type=MESH,
        )

    def joined(own, other, where):
        return 0.5 * (own[where, :].astype(F32) + other[where, :].astype(F32))

    def make_v(level, own, other):
        for part in range(face // CH):
            where = pl.ds(level * face + part * CH, CH)
            v_ref[level, pl.ds(part * CH, CH), :] = joined(own, other, where).astype(BF16)

    places = (3 + box // 2, 1 + box // 4, 0)

    def merge(level, own, other, out, k):
        whole = joined(own, other, rows(k))
        left = whole[:, level * face : (level + 1) * face].astype(BF16)
        inner = inv_ref[places[level]].astype(BF16)
        product = jnp.dot(left, inner, preferred_element_type=F32).astype(BF16)
        out[rows(k), :] = (
            whole - jnp.dot(product, v_ref[level], preferred_element_type=F32)
        ).astype(BF16)

    for k in range(width // CH):
        send(leaf, part0, k, s0, r0, sibling).start()

    @pl.loop(0, width // CH)
    def _(step):
        spot = lax.broadcasted_iota(jnp.int32, (CH, width), 0) + step * CH
        pick[rows(step), :] = (spot == idx_ref[...]).astype(F32).astype(BF16)

    def got(buf, k, ssem, rsem, mate):
        send(buf, buf, k, ssem, rsem, mate).wait_recv()

    for k in range(2):
        got(part0, k, s0, r0, sibling)
    make_v(0, leaf, part0)
    for k in range(2, width // CH):
        got(part0, k, s0, r0, sibling)
    for base in ORDER:
        mine, theirs = base + core, base + 1 - core
        merge(0, leaf, part0, half1, mine)
        send(half1, part1, mine, s1, r1, pair).start()
        merge(0, leaf, part0, half1, theirs)

    def permute(k):
        a_ref[:, rows(k)] = lax.dot_general(
            pick[...], m_ref[rows(k), :], NT, preferred_element_type=F32
        ).astype(BF16)

    def last(step):
        mine, theirs = ORDER[step] + core, ORDER[step] + 1 - core
        got(part2, mine, s2, r2, cross)
        send(part2, part2, mine, q2, r2, sibling).start()
        got(part2, theirs, q2, r2, sibling)
        if step == 0:
            return
        if step == 1:
            make_v(2, half2, part2)
        for other in (0, 1) if step == 1 else (step,):
            for k in (ORDER[other], ORDER[other] + 1):
                merge(2, half2, part2, m_ref, k)
                permute(k)

    for step, base in enumerate(ORDER):
        mine, theirs = base + core, base + 1 - core
        got(part1, mine, s1, r1, pair)
        send(part1, part1, mine, q1, r1, sibling).start()
        if step == 0:
            got(part1, theirs, q1, r1, sibling)
            make_v(1, half1, part1)
        merge(1, half1, part1, half2, mine)
        send(half2, part2, mine, s2, r2, cross).start()
        if step > 0:
            got(part1, theirs, q1, r1, sibling)
        merge(1, half1, part1, half2, theirs)
        if step > 0:
            last(step - 1)
    last(len(ORDER) - 1)

    def dot(x, y):
        return jnp.dot(x, y, preferred_element_type=F32)

    def finite(y):
        return jnp.where(jnp.abs(y) < 1e37, y, 0.0).astype(BF16)

    below, above = jnp.minimum(me + 1, layers - 1), jnp.maximum(me - 1, 0)
    nblk = phi_s.shape[0]
    rb = CH // nblk

    def hop(src, dst, ssem, rsem, where, mate):
        return pltpu.make_async_remote_copy(
            src_ref=src, dst_ref=dst, send_sem=ssem, recv_sem=rsem,
            device_id=(where, mate), device_id_type=MESH,
        )

    def strip(j):
        return pl.ds(j * rb, rb)

    def phi_copy(j):
        return hop(phi.at[strip(j), :], phi_in.at[strip(j), :], phi_s.at[j], phi_r.at[j], below, box)

    def psi_copy(j):
        return hop(psi.at[strip(j), :], psi_in.at[strip(j), :], psi_s.at[j], psi_r.at[j], above, box)

    def res_copy(j):
        return hop(res.at[strip(j), :], res_in.at[strip(j), :], res_s.at[j], res_r.at[j], above, box)

    d_copy = hop(send_d, down_buf, one_s.at[0], one_r.at[0], below, box)
    u_copy = hop(send_u, up_buf, one_s.at[1], one_r.at[1], above, box)

    def own_rows(j):
        return pl.ds(pl.multiple_of(box * CH + j * rb, rb), rb)

    def phi_stream():
        @pl.when(first)
        def _():
            d_ref[...] = src_ref[...]

        @pl.when(jnp.logical_not(first))
        def _():
            d_copy.wait_recv()
            d_ref[...] = src_ref[...] + coupling * dot(down_buf[...], a_ref[...])

        @pl.when(jnp.logical_not(final))
        def _():
            send_d[...] = d_ref[...].astype(BF16)
            d_copy.start()

        @pl.when(final)
        def _():
            send_u[...] = d_ref[...].astype(BF16)
            u_copy.start()

        for j in range(nblk):
            @pl.when(first)
            def _():
                phi[strip(j), :] = (coupling * a_ref[own_rows(j), :].astype(F32)).astype(BF16)

            @pl.when(jnp.logical_not(first))
            def _():
                phi_copy(j).wait_recv()
                phi[strip(j), :] = finite(coupling * dot(phi_in[strip(j), :], a_ref[...]))

            @pl.when(jnp.logical_not(final))
            def _():
                phi_copy(j).start()

            @pl.when(final)
            def _():
                res[strip(j), :] = phi[strip(j), :]
                res_copy(j).start()

    def psi_stream():
        for j in range(nblk):
            @pl.when(final)
            def _():
                psi[strip(j), :] = (coupling * m_ref[own_rows(j), :].astype(F32)).astype(BF16)

            @pl.when(jnp.logical_not(final))
            def _():
                psi_copy(j).wait_recv()
                psi[strip(j), :] = finite(coupling * dot(psi_in[strip(j), :], m_ref[...]))

            @pl.when(jnp.logical_not(first))
            def _():
                psi_copy(j).start()

    @pl.when(z < depth // 2)
    def _():
        phi_stream()
        psi_stream()

    @pl.when(z >= depth // 2)
    def _():
        psi_stream()
        phi_stream()

    def spread(copy_of, begin):
        for step in range(1, depth):
            copy = copy_of(step)
            copy.start() if begin else copy.wait_send()

    def d_spread(step):
        return hop(dcol, dcol, bd_s.at[step], bd_s.at[0],
                   group * depth + lax.rem(z + step, depth), box)

    def u_spread(step):
        return hop(ucol, ucol, bu_s.at[step], bu_s.at[0],
                   group * depth + lax.rem(z + step, depth), box)

    def link_copy(link, buf, ssem, rsem, where, j):
        return hop(link.at[:, :, pl.ds(j * CH, CH)], buf.at[box], ssem.at[j], rsem.at[box], where, j)

    def gather_cols(link, buf, ssem, rsem, col):
        for j in range(boxes):
            hop(buf.at[j], buf.at[j], ssem.at[j], rsem.at[j], me, box).wait_recv()
        total = buf[0]
        for j in range(1, boxes):
            total = total + buf[j]
        for j in range(boxes):
            col16[pl.ds(2 * j, 2), :] = total[j]
        col[...] = col16[...].astype(BF16)

    def unfold(value, link, mine):
        flat[...] = value
        for j in range(boxes):
            part3[j] = flat[pl.ds(2 * j, 2), :]
        if link is not None:
            link[...] = part3[...]
            link[box] += mine

    after = jnp.minimum(group + 1, blocks - 1) * depth + z
    before = jnp.maximum(group - 1, 0) * depth + z

    @pl.when(top)
    def _():
        dcol[...] = jnp.zeros_like(dcol)

    @pl.when(bottom)
    def _():
        ucol[...] = jnp.zeros_like(ucol)

    @pl.when(final)
    def _():
        @pl.when(jnp.logical_not(top))
        def _():
            gather_cols(link_d, in_d, ld_s, ld_r, dcol)
            spread(d_spread, True)

        @pl.when(jnp.logical_not(bottom))
        def _():
            unfold(dot(dcol[...], phi[...]), link_d, d_ref[...])
            for j in range(boxes):
                link_copy(link_d, in_d, ld_s, ld_r, after, j).start()

    @pl.when(final)
    def _():
        u_ref[...] = d_ref[...]

    @pl.when(jnp.logical_not(final))
    def _():
        u_copy.wait_recv()
        u_ref[...] = d_ref[...] + coupling * dot(up_buf[...], m_ref[...])

        @pl.when(jnp.logical_not(first))
        def _():
            send_u[...] = u_ref[...].astype(BF16)
            u_copy.start()

        for j in range(nblk):
            res_copy(j).wait_recv()
            res[strip(j), :] = finite(
                phi[strip(j), :].astype(F32) + coupling * dot(res_in[strip(j), :], m_ref[...])
            )

            @pl.when(jnp.logical_not(first))
            def _():
                res_copy(j).start()

        @pl.when(jnp.logical_not(top))
        def _():
            d_spread(1).wait_recv()

    @pl.when(first)
    def _():
        @pl.when(jnp.logical_not(bottom))
        def _():
            gather_cols(link_u, in_u, lu_s, lu_r, ucol)
            spread(u_spread, True)

        unfold(dot(dcol[...], res[...]) + dot(ucol[...], psi[...]), link_u, u_ref[...])

        @pl.when(jnp.logical_not(top))
        def _():
            for j in range(boxes):
                link_copy(link_u, in_u, lu_s, lu_r, before, j).start()

    @pl.when(jnp.logical_not(first))
    def _():
        @pl.when(jnp.logical_not(bottom))
        def _():
            u_spread(1).wait_recv()

        unfold(dot(dcol[...], res[...]) + dot(ucol[...], psi[...]), None, None)

    def last_copy(step):
        mate = lax.rem(box + step, boxes)
        return hop(part3.at[mate], last_in.at[step], f_s.at[step], f_r.at[step], me, mate)

    for step in range(1, boxes):
        last_copy(step).start()
    total = u_ref[...] + part3[box]
    for step in range(1, boxes):
        last_copy(step).wait_recv()
        total = total + last_in[step]
    out_ref[...] = total

    for step in range(1, boxes):
        last_copy(step).wait_send()

    @pl.when(jnp.logical_not(final))
    def _():
        d_copy.wait_send()
        for j in range(nblk):
            phi_copy(j).wait_send()

    @pl.when(jnp.logical_not(first))
    def _():
        u_copy.wait_send()
        for j in range(nblk):
            psi_copy(j).wait_send()
            res_copy(j).wait_send()

    @pl.when(jnp.logical_and(final, jnp.logical_not(top)))
    def _():
        spread(d_spread, False)

    @pl.when(jnp.logical_and(final, jnp.logical_not(bottom)))
    def _():
        for j in range(boxes):
            link_copy(link_d, in_d, ld_s, ld_r, after, j).wait_send()

    @pl.when(jnp.logical_and(first, jnp.logical_not(bottom)))
    def _():
        spread(u_spread, False)

    @pl.when(jnp.logical_and(first, jnp.logical_not(top)))
    def _():
        for j in range(boxes):
            link_copy(link_u, in_u, lu_s, lu_r, before, j).wait_send()

    for k in range(width // CH):
        send(leaf, part0, k, s0, r0, sibling).wait_send()
    for base in ORDER:
        mine = base + core
        send(half1, part1, mine, s1, r1, pair).wait_send()
        send(half2, part2, mine, s2, r2, cross).wait_send()
        send(part1, part1, mine, q1, r1, sibling).wait_send()
        send(part2, part2, mine, q2, r2, sibling).wait_send()


def on_device(box_maps, block_pattern, face_inverses, index_map, sources):
    boxes = lax.axis_size("box")
    layers = lax.axis_size("layer")
    coupling = math.sqrt(boxes)
    width = box_maps.shape[2]
    rhs = sources.shape[1]
    face = face_inverses.shape[2]
    keep = jnp.repeat(block_pattern[0].astype(F32), width // block_pattern.shape[2], axis=1)
    vmem = pl.BlockSpec(memory_space=pltpu.VMEM)
    square = pltpu.VMEM((width, width), BF16)
    count = pltpu.SemaphoreType.DMA((width // CH,))
    merged, upward = pl.pallas_call(
        functools.partial(kernel, layers, coupling),
        out_shape=(
            jax.ShapeDtypeStruct((width, width), BF16),
            jax.ShapeDtypeStruct((rhs, width), F32),
        ),
        in_specs=[vmem] * 5,
        out_specs=(vmem, vmem),
        scratch_shapes=[square] * 6
        + [pltpu.VMEM((3, face, width), BF16), square, square]
        + [pltpu.VMEM((rhs, width), F32)] * 2
        + [pltpu.VMEM((rhs, width), BF16)] * 4
        + [pltpu.VMEM((CH, width), BF16)] * 6
        + [pltpu.VMEM((boxes * rhs, CH), BF16)] * 2
        + [pltpu.VMEM((boxes * rhs, width), F32)]
        + [pltpu.VMEM((boxes, rhs, width), F32)] * 3
        + [pltpu.VMEM((boxes, boxes, rhs, CH), F32)] * 2
        + [pltpu.VMEM((boxes * rhs, CH), F32), pltpu.VMEM((boxes, rhs, width), F32)]
        + [count] * 8
        + [pltpu.SemaphoreType.DMA((4,))] * 6
        + [pltpu.SemaphoreType.DMA((2,))] * 2
        + [pltpu.SemaphoreType.DMA((boxes,))] * 8,
        compiler_params=pltpu.CompilerParams(
            collective_id=0, has_side_effects=True, vmem_limit_bytes=56 * 2**20
        ),
    )(box_maps[0], keep, face_inverses[0], index_map, sources[0])
    return (merged[None], upward[None])


def solution(mesh):
    return jax.shard_map(
        on_device,
        mesh=mesh,
        in_specs=(
            P("layer", "box", None),
            P("layer", "box", None),
            P("layer", None, None, None),
            P("layer", None),
            P("layer", "box", None),
        ),
        out_specs=(P("layer", None, None), P("layer", "box", None)),
        check_vma=False,
    )
```

```python
import functools
import math

import jax
import jax.numpy as jnp
from jax import lax
from jax.experimental import pallas as pl
from jax.experimental.pallas import tpu as pltpu
from jax.sharding import PartitionSpec as P

MESH = pl.DeviceIdType.MESH
NT = (((1,), (1,)), ((), ()))
F32 = jnp.float32
BF16 = jnp.bfloat16
CH = 128
ORDER = (2, 4, 0, 6)


def kernel(
    layers, coupling, map_hbm, keep_ref, inv_hbm, idx_ref, src_ref,
    m_hbm, out_ref,
    m_ref, part0_in, inv_ref, io_sem,
    leaf, part0, half1, part1, half2, part2, v_ref, pick, a_ref,
    d_ref, u_ref, send_d, send_u, down_buf, up_buf,
    phi, phi_in, psi, psi_in, res, res_in,
    dcol, ucol, flat, part3, link_d, link_u, in_d, in_u, col16, last_in,
    s0, r0, s1, r1, s2, r2, q1, q2,
    phi_s, phi_r, psi_s, psi_r, res_s, res_r, one_s, one_r,
    ld_s, ld_r, lu_s, lu_r, bd_s, bu_s, f_s, f_r,
):
    me = lax.axis_index("layer")
    box = lax.axis_index("box")
    width = m_ref.shape[0]
    face = inv_ref.shape[1]
    places = (3 + box // 2, 1 + box // 4, 0)
    core = lax.rem(box, 2)
    chip = box // 2
    sibling = box + 1 - 2 * core
    pair = 2 * (chip + 1 - 2 * lax.rem(chip, 2)) + core
    cross = 2 * (3 - chip) + core

    depth = 8
    blocks = layers // depth
    boxes = 8
    group = me // depth
    z = lax.rem(me, depth)
    first, final = z == 0, z == depth - 1
    top, bottom = group == 0, group == blocks - 1

    barrier = pltpu.get_barrier_semaphore()

    def greet(layer, mate):
        pl.semaphore_signal(barrier, inc=1, device_id=(layer, mate), device_id_type=MESH)

    for step in range(1, boxes):
        greet(me, lax.rem(box + step, boxes))
    for step in range(1, depth):
        greet(group * depth + lax.rem(z + step, depth), box)
    for step in (1, blocks - 1):
        for mate in range(boxes):
            greet(lax.rem(group + step, blocks) * depth + z, mate)
    def load_map(k):
        return pltpu.make_async_copy(
            map_hbm.at[pl.ds(k * CH, CH), :], part0_in.at[pl.ds(k * CH, CH), :], io_sem.at[k]
        )

    def load_inverse(level):
        return pltpu.make_async_copy(
            inv_hbm.at[places[level]], inv_ref.at[level], io_sem.at[width // CH + level]
        )

    for k in range(width // CH):
        load_map(k).start()
    for level in range(3):
        load_inverse(level).start()
    for k in range(width // CH):
        load_map(k).wait()
        for j in range(width // CH):
            kept = keep_ref[k, j].astype(F32)
            block = (pl.ds(k * CH, CH), pl.ds(j * CH, CH))
            leaf[block] = (part0_in[block].astype(F32) * kept).astype(BF16)
    pl.semaphore_wait(barrier, boxes - 1 + depth - 1 + 2 * boxes)

    def rows(k):
        return pl.ds(pl.multiple_of(k * CH, CH), CH)

    def send(src, dst, k, ssem, rsem, mate):
        return pltpu.make_async_remote_copy(
            src_ref=src.at[rows(k), :], dst_ref=dst.at[rows(k), :],
            send_sem=ssem.at[k], recv_sem=rsem.at[k],
            device_id=(me, mate), device_id_type=MESH,
        )

    def joined(own, other, where):
        return 0.5 * (own[where, :].astype(F32) + other[where, :].astype(F32))

    def make_v(level, own, other):
        for part in range(face // CH):
            where = pl.ds(level * face + part * CH, CH)
            v_ref[level, pl.ds(part * CH, CH), :] = joined(own, other, where).astype(BF16)

    def merge(level, own, other, out, k):
        whole = joined(own, other, rows(k))
        left = whole[:, level * face : (level + 1) * face].astype(BF16)
        inner = inv_ref[level].astype(BF16)
        product = jnp.dot(left, inner, preferred_element_type=F32).astype(BF16)
        out[rows(k), :] = (
            whole - jnp.dot(product, v_ref[level], preferred_element_type=F32)
        ).astype(BF16)

    for k in range(width // CH):
        send(leaf, part0, k, s0, r0, sibling).start()

    @pl.loop(0, width // CH)
    def _(step):
        spot = lax.broadcasted_iota(jnp.int32, (CH, width), 0) + step * CH
        pick[rows(step), :] = (spot == idx_ref[...]).astype(F32).astype(BF16)

    def got(buf, k, ssem, rsem, mate):
        send(buf, buf, k, ssem, rsem, mate).wait_recv()

    for k in range(2):
        got(part0, k, s0, r0, sibling)
    make_v(0, leaf, part0)
    for level in range(3):
        load_inverse(level).wait()
    for base in ORDER:
        mine, theirs = base + core, base + 1 - core
        if base:
            got(part0, mine, s0, r0, sibling)
        merge(0, leaf, part0, half1, mine)
        send(half1, part1, mine, s1, r1, pair).start()
        if base:
            got(part0, theirs, s0, r0, sibling)
        merge(0, leaf, part0, half1, theirs)

    def permute(k):
        a_ref[:, rows(k)] = lax.dot_general(
            pick[...], m_ref[rows(k), :], NT, preferred_element_type=F32
        ).astype(BF16)

    def last(step):
        mine, theirs = ORDER[step] + core, ORDER[step] + 1 - core
        got(part2, mine, s2, r2, cross)
        send(part2, part2, mine, q2, r2, sibling).start()
        got(part2, theirs, q2, r2, sibling)
        if step == 0:
            return
        if step == 1:
            make_v(2, half2, part2)
        for other in (0, 1) if step == 1 else (step,):
            for k in (ORDER[other], ORDER[other] + 1):
                merge(2, half2, part2, m_ref, k)
                permute(k)

    for step, base in enumerate(ORDER):
        mine, theirs = base + core, base + 1 - core
        got(part1, mine, s1, r1, pair)
        send(part1, part1, mine, q1, r1, sibling).start()
        if step == 0:
            got(part1, theirs, q1, r1, sibling)
            make_v(1, half1, part1)
        merge(1, half1, part1, half2, mine)
        send(half2, part2, mine, s2, r2, cross).start()
        if step > 0:
            got(part1, theirs, q1, r1, sibling)
        merge(1, half1, part1, half2, theirs)
        if step > 0:
            last(step - 1)
    last(len(ORDER) - 1)

    store_map = pltpu.make_async_copy(m_ref, m_hbm, io_sem.at[width // CH + 3])
    store_map.start()

    def dot(x, y):
        return jnp.dot(x, y, preferred_element_type=F32)

    def finite(y):
        return jnp.where(jnp.abs(y) < 1e37, y, 0.0).astype(BF16)

    below, above = jnp.minimum(me + 1, layers - 1), jnp.maximum(me - 1, 0)
    nblk = phi_s.shape[0]
    rb = CH // nblk

    def hop(src, dst, ssem, rsem, where, mate):
        return pltpu.make_async_remote_copy(
            src_ref=src, dst_ref=dst, send_sem=ssem, recv_sem=rsem,
            device_id=(where, mate), device_id_type=MESH,
        )

    def strip(j):
        return pl.ds(pl.multiple_of(j * rb, rb), rb)

    def phi_copy(j):
        return hop(phi.at[strip(j), :], phi_in.at[strip(j), :], phi_s.at[j], phi_r.at[j], below, box)

    def psi_copy(j):
        return hop(psi.at[strip(j), :], psi_in.at[strip(j), :], psi_s.at[j], psi_r.at[j], above, box)

    def res_copy(j):
        return hop(res.at[strip(j), :], res_in.at[strip(j), :], res_s.at[j], res_r.at[j], above, box)

    d_copy = hop(send_d, down_buf, one_s.at[0], one_r.at[0], below, box)
    u_copy = hop(send_u, up_buf, one_s.at[1], one_r.at[1], above, box)

    def own_rows(j):
        return pl.ds(pl.multiple_of(box * CH + j * rb, rb), rb)

    def phi_stream():
        @pl.when(first)
        def _():
            d_ref[...] = src_ref[...]

        @pl.when(jnp.logical_not(first))
        def _():
            d_copy.wait_recv()
            d_ref[...] = src_ref[...] + coupling * dot(down_buf[...], a_ref[...])

        @pl.when(jnp.logical_not(final))
        def _():
            send_d[...] = d_ref[...].astype(BF16)
            d_copy.start()

        @pl.when(final)
        def _():
            send_u[...] = d_ref[...].astype(BF16)
            u_copy.start()

        @pl.loop(0, nblk)
        def _(j):
            @pl.when(first)
            def _():
                phi[strip(j), :] = (coupling * a_ref[own_rows(j), :].astype(F32)).astype(BF16)

            @pl.when(jnp.logical_not(first))
            def _():
                phi_copy(j).wait_recv()
                phi[strip(j), :] = finite(coupling * dot(phi_in[strip(j), :], a_ref[...]))

            @pl.when(jnp.logical_not(final))
            def _():
                phi_copy(j).start()

            @pl.when(final)
            def _():
                res[strip(j), :] = phi[strip(j), :]
                res_copy(j).start()

    def psi_stream():
        @pl.loop(0, nblk)
        def _(j):
            @pl.when(final)
            def _():
                psi[strip(j), :] = (coupling * m_ref[own_rows(j), :].astype(F32)).astype(BF16)

            @pl.when(jnp.logical_not(final))
            def _():
                psi_copy(j).wait_recv()
                psi[strip(j), :] = finite(coupling * dot(psi_in[strip(j), :], m_ref[...]))

            @pl.when(jnp.logical_not(first))
            def _():
                psi_copy(j).start()

    @pl.when(z < depth // 2)
    def _():
        phi_stream()
        psi_stream()

    @pl.when(z >= depth // 2)
    def _():
        psi_stream()
        phi_stream()

    def spread(copy_of, begin):
        for step in range(1, depth):
            copy = copy_of(step)
            copy.start() if begin else copy.wait_send()

    def d_spread(step):
        return hop(dcol, dcol, bd_s.at[step], bd_s.at[0],
                   group * depth + lax.rem(z + step, depth), box)

    def u_spread(step):
        return hop(ucol, ucol, bu_s.at[step], bu_s.at[0],
                   group * depth + lax.rem(z + step, depth), box)

    def link_copy(link, buf, ssem, rsem, where, j):
        return hop(link.at[:, :, pl.ds(j * CH, CH)], buf.at[box], ssem.at[j], rsem.at[box], where, j)

    def gather_cols(link, buf, ssem, rsem, col):
        for j in range(boxes):
            hop(buf.at[j], buf.at[j], ssem.at[j], rsem.at[j], me, box).wait_recv()
        total = buf[0]
        for j in range(1, boxes):
            total = total + buf[j]
        for j in range(boxes):
            col16[pl.ds(2 * j, 2), :] = total[j]
        col[...] = col16[...].astype(BF16)

    def unfold(value, link, mine):
        flat[...] = value
        for j in range(boxes):
            part3[j] = flat[pl.ds(2 * j, 2), :]
        if link is not None:
            link[...] = part3[...]
            link[box] += mine

    after = jnp.minimum(group + 1, blocks - 1) * depth + z
    before = jnp.maximum(group - 1, 0) * depth + z

    @pl.when(top)
    def _():
        dcol[...] = jnp.zeros_like(dcol)

    @pl.when(bottom)
    def _():
        ucol[...] = jnp.zeros_like(ucol)

    @pl.when(final)
    def _():
        @pl.when(jnp.logical_not(top))
        def _():
            gather_cols(link_d, in_d, ld_s, ld_r, dcol)
            spread(d_spread, True)

        @pl.when(jnp.logical_not(bottom))
        def _():
            unfold(dot(dcol[...], phi[...]), link_d, d_ref[...])
            for j in range(boxes):
                link_copy(link_d, in_d, ld_s, ld_r, after, j).start()

    @pl.when(final)
    def _():
        u_ref[...] = d_ref[...]

    @pl.when(jnp.logical_not(final))
    def _():
        u_copy.wait_recv()
        u_ref[...] = d_ref[...] + coupling * dot(up_buf[...], m_ref[...])

        @pl.when(jnp.logical_not(first))
        def _():
            send_u[...] = u_ref[...].astype(BF16)
            u_copy.start()

        @pl.loop(0, nblk)
        def _(j):
            res_copy(j).wait_recv()
            res[strip(j), :] = finite(
                phi[strip(j), :].astype(F32) + coupling * dot(res_in[strip(j), :], m_ref[...])
            )

            @pl.when(jnp.logical_not(first))
            def _():
                res_copy(j).start()

        @pl.when(jnp.logical_not(top))
        def _():
            d_spread(1).wait_recv()

    @pl.when(first)
    def _():
        @pl.when(jnp.logical_not(bottom))
        def _():
            gather_cols(link_u, in_u, lu_s, lu_r, ucol)
            spread(u_spread, True)

        unfold(dot(dcol[...], res[...]) + dot(ucol[...], psi[...]), link_u, u_ref[...])

        @pl.when(jnp.logical_not(top))
        def _():
            for j in range(boxes):
                link_copy(link_u, in_u, lu_s, lu_r, before, j).start()

    @pl.when(jnp.logical_not(first))
    def _():
        @pl.when(jnp.logical_not(bottom))
        def _():
            u_spread(1).wait_recv()

        unfold(dot(dcol[...], res[...]) + dot(ucol[...], psi[...]), None, None)

    def last_copy(step):
        mate = lax.rem(box + step, boxes)
        return hop(part3.at[mate], last_in.at[step], f_s.at[step], f_r.at[step], me, mate)

    for step in range(1, boxes):
        last_copy(step).start()
    total = u_ref[...] + part3[box]
    for step in range(1, boxes):
        last_copy(step).wait_recv()
        total = total + last_in[step]
    out_ref[...] = total

    store_map.wait()
    for step in range(1, boxes):
        last_copy(step).wait_send()

    @pl.when(jnp.logical_not(final))
    def _():
        d_copy.wait_send()
        @pl.loop(0, nblk)
        def _(j):
            phi_copy(j).wait_send()

    @pl.when(jnp.logical_not(first))
    def _():
        u_copy.wait_send()
        @pl.loop(0, nblk)
        def _(j):
            psi_copy(j).wait_send()
            res_copy(j).wait_send()

    @pl.when(jnp.logical_and(final, jnp.logical_not(top)))
    def _():
        spread(d_spread, False)

    @pl.when(jnp.logical_and(final, jnp.logical_not(bottom)))
    def _():
        for j in range(boxes):
            link_copy(link_d, in_d, ld_s, ld_r, after, j).wait_send()

    @pl.when(jnp.logical_and(first, jnp.logical_not(bottom)))
    def _():
        spread(u_spread, False)

    @pl.when(jnp.logical_and(first, jnp.logical_not(top)))
    def _():
        for j in range(boxes):
            link_copy(link_u, in_u, lu_s, lu_r, before, j).wait_send()

    for k in range(width // CH):
        send(leaf, part0, k, s0, r0, sibling).wait_send()
    for base in ORDER:
        mine = base + core
        send(half1, part1, mine, s1, r1, pair).wait_send()
        send(half2, part2, mine, s2, r2, cross).wait_send()
        send(part1, part1, mine, q1, r1, sibling).wait_send()
        send(part2, part2, mine, q2, r2, sibling).wait_send()


def hand_on(m_in, u_in, m_out, u_out, m_buf, u_buf, sem):
    count = m_in.shape[0] // CH
    pairs = [(m_in, m_buf, m_out, pl.ds(k * CH, CH)) for k in range(count)]
    pairs.append((u_in, u_buf, u_out, pl.ds(0, u_in.shape[0])))
    loads, stores = [], []
    for k, (src, buf, dst, where) in enumerate(pairs):
        loads.append(pltpu.make_async_copy(src.at[where, :], buf.at[where, :], sem.at[2 * k]))
        stores.append(pltpu.make_async_copy(buf.at[where, :], dst.at[where, :], sem.at[2 * k + 1]))
    for load in loads:
        load.start()
    for load, store in zip(loads, stores):
        load.wait()
        store.start()
    for store in stores:
        store.wait()


def on_device(box_maps, block_pattern, face_inverses, index_map, sources):
    boxes = lax.axis_size("box")
    layers = lax.axis_size("layer")
    coupling = math.sqrt(boxes)
    width = box_maps.shape[2]
    rhs = sources.shape[1]
    face = face_inverses.shape[2]
    vmem = pl.BlockSpec(memory_space=pltpu.VMEM)
    anywhere = pl.BlockSpec(memory_space=pl.ANY)
    square = pltpu.VMEM((width, width), BF16)
    count = pltpu.SemaphoreType.DMA((width // CH,))
    merged, upward = pl.pallas_call(
        functools.partial(kernel, layers, coupling),
        out_shape=(
            jax.ShapeDtypeStruct((width, width), BF16),
            jax.ShapeDtypeStruct((rhs, width), F32),
        ),
        in_specs=[anywhere, pl.BlockSpec(memory_space=pltpu.SMEM), anywhere, vmem, vmem],
        out_specs=(anywhere, vmem),
        scratch_shapes=[
            square, square, pltpu.VMEM((3, face, face), F32), pltpu.SemaphoreType.DMA((16,)),
        ]
        + [square] * 6
        + [pltpu.VMEM((3, face, width), BF16), square, square]
        + [pltpu.VMEM((rhs, width), F32)] * 2
        + [pltpu.VMEM((rhs, width), BF16)] * 4
        + [pltpu.VMEM((CH, width), BF16)] * 6
        + [pltpu.VMEM((boxes * rhs, CH), BF16)] * 2
        + [pltpu.VMEM((boxes * rhs, width), F32)]
        + [pltpu.VMEM((boxes, rhs, width), F32)] * 3
        + [pltpu.VMEM((boxes, boxes, rhs, CH), F32)] * 2
        + [pltpu.VMEM((boxes * rhs, CH), F32), pltpu.VMEM((boxes, rhs, width), F32)]
        + [count] * 8
        + [pltpu.SemaphoreType.DMA((8,))] * 6
        + [pltpu.SemaphoreType.DMA((2,))] * 2
        + [pltpu.SemaphoreType.DMA((boxes,))] * 8,
        compiler_params=pltpu.CompilerParams(
            collective_id=0, has_side_effects=True, vmem_limit_bytes=56 * 2**20
        ),
    )(box_maps[0], block_pattern[0], face_inverses[0], index_map, sources[0])
    merged, upward = pl.pallas_call(
        hand_on,
        out_shape=(
            jax.ShapeDtypeStruct((width, width), BF16),
            jax.ShapeDtypeStruct((rhs, width), F32),
        ),
        in_specs=[anywhere, anywhere],
        out_specs=(anywhere, anywhere),
        scratch_shapes=[
            square, pltpu.VMEM((rhs, width), F32), pltpu.SemaphoreType.DMA((18,)),
        ],
    )(merged, upward)
    return (merged[None], upward[None])


def solution(mesh):
    return jax.shard_map(
        on_device,
        mesh=mesh,
        in_specs=(
            P("layer", "box", None),
            P("layer", "box", None),
            P("layer", None, None, None),
            P("layer", None),
            P("layer", "box", None),
        ),
        out_specs=(P("layer", None, None), P("layer", "box", None)),
        check_vma=False,
    )
```

```python
import functools
import math

import jax
import jax.numpy as jnp
from jax import lax
from jax.experimental import pallas as pl
from jax.experimental.pallas import tpu as pltpu
from jax.sharding import PartitionSpec as P

MESH = pl.DeviceIdType.MESH
NT = (((1,), (1,)), ((), ()))
F32 = jnp.float32
BF16 = jnp.bfloat16
CH = 128
ORDER = (2, 4, 0, 6)


def kernel(
    layers, coupling, map_hbm, keep_ref, inv_hbm, idx_ref, src_ref,
    m_hbm, out_ref,
    m_ref, part0_in, inv_ref, io_sem,
    leaf, part0, half1, part1, half2, part2, v_ref, pick, a_ref,
    d_ref, u_ref, send_d, send_u, down_buf, up_buf,
    phi, phi_in, psi, psi_in, res, res_in,
    dcol, ucol, flat, part3, link_d, link_u, in_d, in_u, wide, last_in,
    s0, r0, s1, r1, s2, r2, q1, q2,
    phi_s, phi_r, psi_s, psi_r, res_s, res_r, one_s, one_r,
    ld_s, ld_r, lu_s, lu_r, bd_s, bu_s, f_s, f_r,
):
    me = lax.axis_index("layer")
    box = lax.axis_index("box")
    width = m_ref.shape[0]
    face = inv_ref.shape[1]
    places = (3 + box // 2, 1 + box // 4, 0)
    core = lax.rem(box, 2)
    chip = box // 2
    sibling = box + 1 - 2 * core
    pair = 2 * (chip + 1 - 2 * lax.rem(chip, 2)) + core
    cross = 2 * (3 - chip) + core

    depth = 8
    blocks = layers // depth
    boxes = 8
    group = me // depth
    z = lax.rem(me, depth)
    first, final = z == 0, z == depth - 1
    top, bottom = group == 0, group == blocks - 1

    barrier = pltpu.get_barrier_semaphore()

    def greet(layer, mate):
        pl.semaphore_signal(barrier, inc=1, device_id=(layer, mate), device_id_type=MESH)

    for step in range(1, boxes):
        greet(me, lax.rem(box + step, boxes))
    for step in range(1, depth):
        greet(group * depth + lax.rem(z + step, depth), box)
    for step in (1, blocks - 1):
        for mate in range(boxes):
            greet(lax.rem(group + step, blocks) * depth + z, mate)
    def load_map(k):
        return pltpu.make_async_copy(
            map_hbm.at[pl.ds(k * CH, CH), :], part0_in.at[pl.ds(k * CH, CH), :], io_sem.at[k]
        )

    def load_inverse(level):
        return pltpu.make_async_copy(
            inv_hbm.at[places[level]], inv_ref.at[level], io_sem.at[width // CH + level]
        )

    for k in range(width // CH):
        load_map(k).start()
    for level in range(3):
        load_inverse(level).start()
    @pl.loop(0, width // CH)
    def _(step):
        spot = lax.broadcasted_iota(jnp.int32, (CH, width), 0) + step * CH
        pick[pl.ds(pl.multiple_of(step * CH, CH), CH), :] = (spot == idx_ref[...]).astype(F32).astype(BF16)

    for k in range(width // CH):
        load_map(k).wait()
        for j in range(width // CH):
            kept = keep_ref[k, j].astype(F32)
            block = (pl.ds(k * CH, CH), pl.ds(j * CH, CH))
            leaf[block] = (part0_in[block].astype(F32) * kept).astype(BF16)
    pl.semaphore_wait(barrier, boxes - 1 + depth - 1 + 2 * boxes)

    def rows(k):
        return pl.ds(pl.multiple_of(k * CH, CH), CH)

    def send(src, dst, k, ssem, rsem, mate):
        return pltpu.make_async_remote_copy(
            src_ref=src.at[rows(k), :], dst_ref=dst.at[rows(k), :],
            send_sem=ssem.at[k], recv_sem=rsem.at[k],
            device_id=(me, mate), device_id_type=MESH,
        )

    def joined(own, other, where):
        return 0.5 * (own[where, :].astype(F32) + other[where, :].astype(F32))

    def make_v(level, own, other):
        for part in range(face // CH):
            where = pl.ds(level * face + part * CH, CH)
            v_ref[level, pl.ds(part * CH, CH), :] = joined(own, other, where).astype(BF16)

    def merge(level, own, other, out, k):
        whole = joined(own, other, rows(k))
        left = whole[:, level * face : (level + 1) * face].astype(BF16)
        inner = inv_ref[level].astype(BF16)
        product = jnp.dot(left, inner, preferred_element_type=F32).astype(BF16)
        out[rows(k), :] = (
            whole - jnp.dot(product, v_ref[level], preferred_element_type=F32)
        ).astype(BF16)

    for k in range(width // CH):
        send(leaf, part0, k, s0, r0, sibling).start()

    def got(buf, k, ssem, rsem, mate):
        send(buf, buf, k, ssem, rsem, mate).wait_recv()

    for k in range(2):
        got(part0, k, s0, r0, sibling)
    make_v(0, leaf, part0)
    for level in range(3):
        load_inverse(level).wait()
    for base in ORDER:
        mine, theirs = base + core, base + 1 - core
        if base:
            got(part0, mine, s0, r0, sibling)
        merge(0, leaf, part0, half1, mine)
        send(half1, part1, mine, s1, r1, pair).start()
        if base:
            got(part0, theirs, s0, r0, sibling)
        merge(0, leaf, part0, half1, theirs)

    def permute(k):
        a_ref[:, rows(k)] = lax.dot_general(
            pick[...], m_ref[rows(k), :], NT, preferred_element_type=F32
        ).astype(BF16)

    def last(step):
        mine, theirs = ORDER[step] + core, ORDER[step] + 1 - core
        got(part2, mine, s2, r2, cross)
        send(part2, part2, mine, q2, r2, sibling).start()
        if step > 1:
            merge(2, half2, part2, m_ref, mine)
            permute(mine)
        got(part2, theirs, q2, r2, sibling)
        if step == 0:
            return
        if step > 1:
            merge(2, half2, part2, m_ref, theirs)
            permute(theirs)
            return
        make_v(2, half2, part2)
        for k in (ORDER[0], ORDER[0] + 1, ORDER[1], ORDER[1] + 1):
            merge(2, half2, part2, m_ref, k)
            permute(k)

    for step, base in enumerate(ORDER):
        mine, theirs = base + core, base + 1 - core
        got(part1, mine, s1, r1, pair)
        send(part1, part1, mine, q1, r1, sibling).start()
        if step == 0:
            got(part1, theirs, q1, r1, sibling)
            make_v(1, half1, part1)
        merge(1, half1, part1, half2, mine)
        send(half2, part2, mine, s2, r2, cross).start()
        if step > 0:
            got(part1, theirs, q1, r1, sibling)
        merge(1, half1, part1, half2, theirs)
        if step > 0:
            last(step - 1)
    last(len(ORDER) - 1)

    store_map = pltpu.make_async_copy(m_ref, m_hbm, io_sem.at[width // CH + 3])
    store_map.start()

    def dot(x, y):
        return jnp.dot(x, y, preferred_element_type=F32)

    def finite(y):
        return jnp.where(jnp.abs(y) < 1e37, y, 0.0).astype(BF16)

    below, above = jnp.minimum(me + 1, layers - 1), jnp.maximum(me - 1, 0)
    nblk = phi_s.shape[0]
    rb = CH // nblk

    def hop(src, dst, ssem, rsem, where, mate):
        return pltpu.make_async_remote_copy(
            src_ref=src, dst_ref=dst, send_sem=ssem, recv_sem=rsem,
            device_id=(where, mate), device_id_type=MESH,
        )

    def strip(j):
        return pl.ds(pl.multiple_of(j * rb, rb), rb)

    def phi_copy(j):
        return hop(phi.at[strip(j), :], phi_in.at[strip(j), :], phi_s.at[j], phi_r.at[j], below, box)

    def psi_copy(j):
        return hop(psi.at[strip(j), :], psi_in.at[strip(j), :], psi_s.at[j], psi_r.at[j], above, box)

    def res_copy(j):
        return hop(res.at[strip(j), :], res_in.at[strip(j), :], res_s.at[j], res_r.at[j], above, box)

    d_copy = hop(send_d, down_buf, one_s.at[0], one_r.at[0], below, box)
    u_copy = hop(send_u, up_buf, one_s.at[1], one_r.at[1], above, box)

    def own_rows(j):
        return pl.ds(pl.multiple_of(box * CH + j * rb, rb), rb)

    def phi_stream():
        @pl.when(first)
        def _():
            d_ref[...] = src_ref[...]

        @pl.when(jnp.logical_not(first))
        def _():
            d_copy.wait_recv()
            d_ref[...] = src_ref[...] + coupling * dot(down_buf[...], a_ref[...])

        @pl.when(jnp.logical_not(final))
        def _():
            send_d[...] = d_ref[...].astype(BF16)
            d_copy.start()

        @pl.when(final)
        def _():
            send_u[...] = d_ref[...].astype(BF16)
            u_copy.start()

        @pl.loop(0, nblk)
        def _(j):
            @pl.when(first)
            def _():
                phi[strip(j), :] = (coupling * a_ref[own_rows(j), :].astype(F32)).astype(BF16)

            @pl.when(jnp.logical_not(first))
            def _():
                phi_copy(j).wait_recv()
                phi[strip(j), :] = finite(coupling * dot(phi_in[strip(j), :], a_ref[...]))

            @pl.when(jnp.logical_not(final))
            def _():
                phi_copy(j).start()

            @pl.when(final)
            def _():
                res[strip(j), :] = phi[strip(j), :]
                res_copy(j).start()

    def psi_stream():
        @pl.loop(0, nblk)
        def _(j):
            @pl.when(final)
            def _():
                psi[strip(j), :] = (coupling * m_ref[own_rows(j), :].astype(F32)).astype(BF16)

            @pl.when(jnp.logical_not(final))
            def _():
                psi_copy(j).wait_recv()
                psi[strip(j), :] = finite(coupling * dot(psi_in[strip(j), :], m_ref[...]))

            @pl.when(jnp.logical_not(first))
            def _():
                psi_copy(j).start()

    @pl.when(z < depth // 2)
    def _():
        phi_stream()
        psi_stream()

    @pl.when(z >= depth // 2)
    def _():
        psi_stream()
        phi_stream()

    def spread(copy_of, begin):
        for step in range(1, depth):
            copy = copy_of(step)
            copy.start() if begin else copy.wait_send()

    def d_spread(step):
        return hop(dcol, dcol, bd_s.at[step], bd_s.at[0],
                   group * depth + lax.rem(z + step, depth), box)

    def u_spread(step):
        return hop(ucol, ucol, bu_s.at[step], bu_s.at[0],
                   group * depth + lax.rem(z + step, depth), box)

    def link_copy(link, buf, ssem, rsem, where, j):
        return hop(link.at[:, pl.ds(j * CH, CH)], buf.at[box], ssem.at[j], rsem.at[box], where, j)

    def gather_cols(link, buf, ssem, rsem, col):
        for j in range(boxes):
            hop(buf.at[j], buf.at[j], ssem.at[j], rsem.at[j], me, box).wait_recv()
        total = buf[0].astype(F32)
        for j in range(1, boxes):
            total = total + buf[j].astype(F32)
        col[...] = total.astype(BF16)

    def make_link(value, link, mine):
        for j in range(boxes):
            wide[pl.ds(2 * j, 2), :] = mine
        row = lax.broadcasted_iota(jnp.int32, wide.shape, 0) - 2 * box
        own = jnp.logical_and(row >= 0, row < 2)
        link[...] = (value + jnp.where(own, wide[...], 0.0)).astype(BF16)

    after = jnp.minimum(group + 1, blocks - 1) * depth + z
    before = jnp.maximum(group - 1, 0) * depth + z

    @pl.when(top)
    def _():
        dcol[...] = jnp.zeros_like(dcol)

    @pl.when(bottom)
    def _():
        ucol[...] = jnp.zeros_like(ucol)

    @pl.when(final)
    def _():
        @pl.when(jnp.logical_not(top))
        def _():
            gather_cols(link_d, in_d, ld_s, ld_r, dcol)
            spread(d_spread, True)

        @pl.when(jnp.logical_not(bottom))
        def _():
            make_link(dot(dcol[...], phi[...]), link_d, d_ref[...])
            for j in range(boxes):
                link_copy(link_d, in_d, ld_s, ld_r, after, j).start()

    @pl.when(final)
    def _():
        u_ref[...] = d_ref[...]

    @pl.when(jnp.logical_not(final))
    def _():
        u_copy.wait_recv()
        u_ref[...] = d_ref[...] + coupling * dot(up_buf[...], m_ref[...])

        @pl.when(jnp.logical_not(first))
        def _():
            send_u[...] = u_ref[...].astype(BF16)
            u_copy.start()

        @pl.loop(0, nblk)
        def _(j):
            res_copy(j).wait_recv()
            res[strip(j), :] = finite(
                phi[strip(j), :].astype(F32) + coupling * dot(res_in[strip(j), :], m_ref[...])
            )

            @pl.when(jnp.logical_not(first))
            def _():
                res_copy(j).start()

        @pl.when(jnp.logical_not(top))
        def _():
            d_spread(1).wait_recv()

    flat[...] = dot(dcol[...], res[...])

    @pl.when(first)
    def _():
        @pl.when(jnp.logical_not(bottom))
        def _():
            gather_cols(link_u, in_u, lu_s, lu_r, ucol)
            spread(u_spread, True)

        flat[...] += dot(ucol[...], psi[...])

        @pl.when(jnp.logical_not(top))
        def _():
            make_link(flat[...], link_u, u_ref[...])
            for j in range(boxes):
                link_copy(link_u, in_u, lu_s, lu_r, before, j).start()

    @pl.when(jnp.logical_not(first))
    def _():
        @pl.when(jnp.logical_not(bottom))
        def _():
            u_spread(1).wait_recv()

        flat[...] += dot(ucol[...], psi[...])

    for j in range(boxes):
        part3[j] = flat[pl.ds(2 * j, 2), :].astype(BF16)

    def last_copy(step):
        mate = lax.rem(box + step, boxes)
        return hop(part3.at[mate], last_in.at[step], f_s.at[step], f_r.at[step], me, mate)

    for step in range(1, boxes):
        last_copy(step).start()
    total = u_ref[...] + part3[box].astype(F32)
    for step in range(1, boxes):
        last_copy(step).wait_recv()
        total = total + last_in[step].astype(F32)
    out_ref[...] = total

    store_map.wait()
    for step in range(1, boxes):
        last_copy(step).wait_send()

    @pl.when(jnp.logical_not(final))
    def _():
        d_copy.wait_send()
        @pl.loop(0, nblk)
        def _(j):
            phi_copy(j).wait_send()

    @pl.when(jnp.logical_not(first))
    def _():
        u_copy.wait_send()
        @pl.loop(0, nblk)
        def _(j):
            psi_copy(j).wait_send()
            res_copy(j).wait_send()

    @pl.when(jnp.logical_and(final, jnp.logical_not(top)))
    def _():
        spread(d_spread, False)

    @pl.when(jnp.logical_and(final, jnp.logical_not(bottom)))
    def _():
        for j in range(boxes):
            link_copy(link_d, in_d, ld_s, ld_r, after, j).wait_send()

    @pl.when(jnp.logical_and(first, jnp.logical_not(bottom)))
    def _():
        spread(u_spread, False)

    @pl.when(jnp.logical_and(first, jnp.logical_not(top)))
    def _():
        for j in range(boxes):
            link_copy(link_u, in_u, lu_s, lu_r, before, j).wait_send()

    for k in range(width // CH):
        send(leaf, part0, k, s0, r0, sibling).wait_send()
    for base in ORDER:
        mine = base + core
        send(half1, part1, mine, s1, r1, pair).wait_send()
        send(half2, part2, mine, s2, r2, cross).wait_send()
        send(part1, part1, mine, q1, r1, sibling).wait_send()
        send(part2, part2, mine, q2, r2, sibling).wait_send()


def hand_on(m_in, u_in, m_out, u_out, m_buf, u_buf, sem):
    count = m_in.shape[0] // CH
    pairs = [(m_in, m_buf, m_out, pl.ds(k * CH, CH)) for k in range(count)]
    pairs.append((u_in, u_buf, u_out, pl.ds(0, u_in.shape[0])))
    loads, stores = [], []
    for k, (src, buf, dst, where) in enumerate(pairs):
        loads.append(pltpu.make_async_copy(src.at[where, :], buf.at[where, :], sem.at[2 * k]))
        stores.append(pltpu.make_async_copy(buf.at[where, :], dst.at[where, :], sem.at[2 * k + 1]))
    for load in loads:
        load.start()
    for load, store in zip(loads, stores):
        load.wait()
        store.start()
    for store in stores:
        store.wait()


def on_device(box_maps, block_pattern, face_inverses, index_map, sources):
    boxes = lax.axis_size("box")
    layers = lax.axis_size("layer")
    coupling = math.sqrt(boxes)
    width = box_maps.shape[2]
    rhs = sources.shape[1]
    face = face_inverses.shape[2]
    vmem = pl.BlockSpec(memory_space=pltpu.VMEM)
    anywhere = pl.BlockSpec(memory_space=pl.ANY)
    square = pltpu.VMEM((width, width), BF16)
    count = pltpu.SemaphoreType.DMA((width // CH,))
    merged, upward = pl.pallas_call(
        functools.partial(kernel, layers, coupling),
        out_shape=(
            jax.ShapeDtypeStruct((width, width), BF16),
            jax.ShapeDtypeStruct((rhs, width), F32),
        ),
        in_specs=[anywhere, pl.BlockSpec(memory_space=pltpu.SMEM), anywhere, vmem, vmem],
        out_specs=(anywhere, vmem),
        scratch_shapes=[
            square, square, pltpu.VMEM((3, face, face), F32), pltpu.SemaphoreType.DMA((16,)),
        ]
        + [square] * 6
        + [pltpu.VMEM((3, face, width), BF16), square, square]
        + [pltpu.VMEM((rhs, width), F32)] * 2
        + [pltpu.VMEM((rhs, width), BF16)] * 4
        + [pltpu.VMEM((CH, width), BF16)] * 6
        + [pltpu.VMEM((boxes * rhs, CH), BF16)] * 2
        + [pltpu.VMEM((boxes * rhs, width), F32)]
        + [pltpu.VMEM((boxes, rhs, width), BF16)]
        + [pltpu.VMEM((boxes * rhs, width), BF16)] * 2
        + [pltpu.VMEM((boxes, boxes * rhs, CH), BF16)] * 2
        + [pltpu.VMEM((boxes * rhs, width), F32), pltpu.VMEM((boxes, rhs, width), BF16)]
        + [count] * 8
        + [pltpu.SemaphoreType.DMA((8,))] * 6
        + [pltpu.SemaphoreType.DMA((2,))] * 2
        + [pltpu.SemaphoreType.DMA((boxes,))] * 8,
        compiler_params=pltpu.CompilerParams(
            collective_id=0, has_side_effects=True, vmem_limit_bytes=56 * 2**20
        ),
    )(box_maps[0], block_pattern[0], face_inverses[0], index_map, sources[0])
    merged, upward = pl.pallas_call(
        hand_on,
        out_shape=(
            jax.ShapeDtypeStruct((width, width), BF16),
            jax.ShapeDtypeStruct((rhs, width), F32),
        ),
        in_specs=[anywhere, anywhere],
        out_specs=(anywhere, anywhere),
        scratch_shapes=[
            square, pltpu.VMEM((rhs, width), F32), pltpu.SemaphoreType.DMA((18,)),
        ],
    )(merged, upward)
    return (merged[None], upward[None])


def solution(mesh):
    return jax.shard_map(
        on_device,
        mesh=mesh,
        in_specs=(
            P("layer", "box", None),
            P("layer", "box", None),
            P("layer", None, None, None),
            P("layer", None),
            P("layer", "box", None),
        ),
        out_specs=(P("layer", None, None), P("layer", "box", None)),
        check_vma=False,
    )
```

```python
import functools
import math

import jax
import jax.numpy as jnp
from jax import lax
from jax.experimental import pallas as pl
from jax.experimental.pallas import tpu as pltpu
from jax.sharding import PartitionSpec as P

MESH = pl.DeviceIdType.MESH
NT = (((1,), (1,)), ((), ()))
F32 = jnp.float32
BF16 = jnp.bfloat16
CH = 128
ORDER = (2, 4, 0, 6)


def kernel(
    layers, coupling, map_hbm, keep_ref, inv_hbm, idx_ref, src_ref,
    m_hbm, out_ref,
    m_ref, part0_in, inv_ref, io_sem,
    leaf, part0, half1, part1, half2, part2, v_ref, pick, a_ref,
    d_ref, u_ref, send_d, send_u, down_buf, up_buf,
    phi, phi_in, psi, psi_in, res, res_in,
    dcol, ucol, flat, part3, link_d, link_u, in_d, in_u, wide, last_in,
    s0, r0, s1, r1, s2, r2, q1, q2,
    phi_s, phi_r, psi_s, psi_r, res_s, res_r, one_s, one_r,
    ld_s, ld_r, lu_s, lu_r, bd_s, bu_s, f_s, f_r,
):
    me = lax.axis_index("layer")
    box = lax.axis_index("box")
    width = m_ref.shape[0]
    face = inv_ref.shape[1]
    places = (3 + box // 2, 1 + box // 4, 0)
    core = lax.rem(box, 2)
    chip = box // 2
    parity = lax.rem(chip, 2)
    sibling = box + 1 - 2 * core
    pair = 2 * (chip + 1 - 2 * lax.rem(chip, 2)) + core
    cross = 2 * (3 - chip) + core

    depth = 8
    blocks = layers // depth
    boxes = 8
    group = me // depth
    z = lax.rem(me, depth)
    first, final = z == 0, z == depth - 1
    top, bottom = group == 0, group == blocks - 1

    barrier = pltpu.get_barrier_semaphore()

    def greet(layer, mate):
        pl.semaphore_signal(barrier, inc=1, device_id=(layer, mate), device_id_type=MESH)

    for step in range(1, boxes):
        greet(me, lax.rem(box + step, boxes))
    for step in range(1, depth):
        greet(group * depth + lax.rem(z + step, depth), box)
    for step in (1, blocks - 1):
        for mate in range(boxes):
            greet(lax.rem(group + step, blocks) * depth + z, mate)
    def load_map(k):
        return pltpu.make_async_copy(
            map_hbm.at[pl.ds(k * CH, CH), :], part0_in.at[pl.ds(k * CH, CH), :], io_sem.at[k]
        )

    def load_inverse(level):
        return pltpu.make_async_copy(
            inv_hbm.at[places[level]], inv_ref.at[level], io_sem.at[width // CH + level]
        )

    for k in range(width // CH):
        load_map(k).start()
    for level in range(3):
        load_inverse(level).start()
    @pl.loop(0, width // CH)
    def _(step):
        spot = lax.broadcasted_iota(jnp.int32, (CH, width), 0) + step * CH
        pick[pl.ds(pl.multiple_of(step * CH, CH), CH), :] = (spot == idx_ref[...]).astype(F32).astype(BF16)

    for k in range(width // CH):
        load_map(k).wait()
        for j in range(width // CH):
            kept = keep_ref[k, j].astype(F32)
            block = (pl.ds(k * CH, CH), pl.ds(j * CH, CH))
            leaf[block] = (part0_in[block].astype(F32) * kept).astype(BF16)
    pl.semaphore_wait(barrier, boxes - 1 + depth - 1 + 2 * boxes)

    def rows(k):
        return pl.ds(pl.multiple_of(k * CH, CH), CH)

    def send(src, dst, k, ssem, rsem, mate):
        return pltpu.make_async_remote_copy(
            src_ref=src.at[rows(k), :], dst_ref=dst.at[rows(k), :],
            send_sem=ssem.at[k], recv_sem=rsem.at[k],
            device_id=(me, mate), device_id_type=MESH,
        )

    def joined(own, other, where):
        return 0.5 * (own[where, :].astype(F32) + other[where, :].astype(F32))

    def make_v(level, own, other):
        for part in range(face // CH):
            where = pl.ds(level * face + part * CH, CH)
            v_ref[level, pl.ds(part * CH, CH), :] = joined(own, other, where).astype(BF16)

    def merge(level, own, other, out, k):
        whole = joined(own, other, rows(k))
        left = whole[:, level * face : (level + 1) * face].astype(BF16)
        inner = inv_ref[level].astype(BF16)
        product = jnp.dot(left, inner, preferred_element_type=F32).astype(BF16)
        out[rows(k), :] = (
            whole - jnp.dot(product, v_ref[level], preferred_element_type=F32)
        ).astype(BF16)

    for k in range(width // CH):
        send(leaf, part0, k, s0, r0, sibling).start()

    def got(buf, k, ssem, rsem, mate):
        send(buf, buf, k, ssem, rsem, mate).wait_recv()

    for k in range(2):
        got(part0, k, s0, r0, sibling)
    make_v(0, leaf, part0)
    for level in range(3):
        load_inverse(level).wait()
    for base in ORDER:
        mine, theirs = base + core, base + 1 - core
        if base:
            got(part0, mine, s0, r0, sibling)
        merge(0, leaf, part0, half1, mine)
        send(half1, part1, mine, s1, r1, pair).start()
        if base:
            got(part0, theirs, s0, r0, sibling)
        merge(0, leaf, part0, half1, theirs)

    def permute(k):
        a_ref[:, rows(k)] = lax.dot_general(
            pick[...], m_ref[rows(k), :], NT, preferred_element_type=F32
        ).astype(BF16)

    def last(step):
        mine, theirs = ORDER[step] + core, ORDER[step] + 1 - core
        got(part2, mine, s2, r2, cross)
        if step == 2:
            pl.when(core != parity)(send(part2, part2, mine, s2, r2, pair).start)
        send(part2, part2, mine, q2, r2, sibling).start()
        if step > 1:
            merge(2, half2, part2, m_ref, mine)
            permute(mine)
        got(part2, theirs, q2, r2, sibling)
        if step == 0:
            return
        if step > 1:
            merge(2, half2, part2, m_ref, theirs)
            permute(theirs)
            return
        make_v(2, half2, part2)
        for k in (ORDER[0], ORDER[0] + 1, ORDER[1], ORDER[1] + 1):
            merge(2, half2, part2, m_ref, k)
            permute(k)

    for step, base in enumerate(ORDER):
        mine, theirs = base + core, base + 1 - core
        got(part1, mine, s1, r1, pair)
        send(part1, part1, mine, q1, r1, sibling).start()
        if step == 0:
            got(part1, theirs, q1, r1, sibling)
            make_v(1, half1, part1)
        merge(1, half1, part1, half2, mine)
        if step == 2:
            pl.when(core == parity)(send(half2, part2, mine, s2, r2, cross).start)
        else:
            send(half2, part2, mine, s2, r2, cross).start()
        if step > 0:
            got(part1, theirs, q1, r1, sibling)
        merge(1, half1, part1, half2, theirs)
        if step > 0:
            last(step - 1)
    last(len(ORDER) - 1)

    store_map = pltpu.make_async_copy(m_ref, m_hbm, io_sem.at[width // CH + 3])
    store_map.start()

    def dot(x, y):
        return jnp.dot(x, y, preferred_element_type=F32)

    def finite(y):
        return jnp.where(jnp.abs(y) < 1e37, y, 0.0).astype(BF16)

    below, above = jnp.minimum(me + 1, layers - 1), jnp.maximum(me - 1, 0)
    nblk = phi_s.shape[0]
    rb = CH // nblk

    def hop(src, dst, ssem, rsem, where, mate):
        return pltpu.make_async_remote_copy(
            src_ref=src, dst_ref=dst, send_sem=ssem, recv_sem=rsem,
            device_id=(where, mate), device_id_type=MESH,
        )

    def strip(j):
        return pl.ds(pl.multiple_of(j * rb, rb), rb)

    def phi_copy(j):
        return hop(phi.at[strip(j), :], phi_in.at[strip(j), :], phi_s.at[j], phi_r.at[j], below, box)

    def psi_copy(j):
        return hop(psi.at[strip(j), :], psi_in.at[strip(j), :], psi_s.at[j], psi_r.at[j], above, box)

    def res_copy(j):
        return hop(res.at[strip(j), :], res_in.at[strip(j), :], res_s.at[j], res_r.at[j], above, box)

    d_copy = hop(send_d, down_buf, one_s.at[0], one_r.at[0], below, box)
    u_copy = hop(send_u, up_buf, one_s.at[1], one_r.at[1], above, box)

    def own_rows(j):
        return pl.ds(pl.multiple_of(box * CH + j * rb, rb), rb)

    def phi_stream():
        @pl.when(first)
        def _():
            d_ref[...] = src_ref[...]

        @pl.when(jnp.logical_not(first))
        def _():
            d_copy.wait_recv()
            d_ref[...] = src_ref[...] + coupling * dot(down_buf[...], a_ref[...])

        @pl.when(jnp.logical_not(final))
        def _():
            send_d[...] = d_ref[...].astype(BF16)
            d_copy.start()

        @pl.when(final)
        def _():
            send_u[...] = d_ref[...].astype(BF16)
            u_copy.start()

        @pl.loop(0, nblk)
        def _(j):
            @pl.when(first)
            def _():
                phi[strip(j), :] = (coupling * a_ref[own_rows(j), :].astype(F32)).astype(BF16)

            @pl.when(jnp.logical_not(first))
            def _():
                phi_copy(j).wait_recv()
                phi[strip(j), :] = finite(coupling * dot(phi_in[strip(j), :], a_ref[...]))

            @pl.when(jnp.logical_not(final))
            def _():
                phi_copy(j).start()

            @pl.when(final)
            def _():
                res[strip(j), :] = phi[strip(j), :]
                res_copy(j).start()

    def psi_stream():
        @pl.loop(0, nblk)
        def _(j):
            @pl.when(final)
            def _():
                psi[strip(j), :] = (coupling * m_ref[own_rows(j), :].astype(F32)).astype(BF16)

            @pl.when(jnp.logical_not(final))
            def _():
                psi_copy(j).wait_recv()
                psi[strip(j), :] = finite(coupling * dot(psi_in[strip(j), :], m_ref[...]))

            @pl.when(jnp.logical_not(first))
            def _():
                psi_copy(j).start()

    @pl.when(z < depth // 2)
    def _():
        phi_stream()
        psi_stream()

    @pl.when(z >= depth // 2)
    def _():
        psi_stream()
        phi_stream()

    def spread(copy_of, begin):
        for step in range(1, depth):
            copy = copy_of(step)
            copy.start() if begin else copy.wait_send()

    def d_spread(step):
        return hop(dcol, dcol, bd_s.at[step], bd_s.at[0],
                   group * depth + lax.rem(z + step, depth), box)

    def u_spread(step):
        return hop(ucol, ucol, bu_s.at[step], bu_s.at[0],
                   group * depth + lax.rem(z + step, depth), box)

    def link_copy(link, buf, ssem, rsem, where, j):
        return hop(link.at[:, pl.ds(j * CH, CH)], buf.at[box], ssem.at[j], rsem.at[box], where, j)

    def gather_cols(link, buf, ssem, rsem, col):
        for j in range(boxes):
            hop(buf.at[j], buf.at[j], ssem.at[j], rsem.at[j], me, box).wait_recv()
        total = buf[0].astype(F32)
        for j in range(1, boxes):
            total = total + buf[j].astype(F32)
        col[...] = total.astype(BF16)

    def make_link(value, link, mine):
        for j in range(boxes):
            wide[pl.ds(2 * j, 2), :] = mine
        row = lax.broadcasted_iota(jnp.int32, wide.shape, 0) - 2 * box
        own = jnp.logical_and(row >= 0, row < 2)
        link[...] = (value + jnp.where(own, wide[...], 0.0)).astype(BF16)

    after = jnp.minimum(group + 1, blocks - 1) * depth + z
    before = jnp.maximum(group - 1, 0) * depth + z

    @pl.when(top)
    def _():
        dcol[...] = jnp.zeros_like(dcol)

    @pl.when(bottom)
    def _():
        ucol[...] = jnp.zeros_like(ucol)

    @pl.when(final)
    def _():
        @pl.when(jnp.logical_not(top))
        def _():
            gather_cols(link_d, in_d, ld_s, ld_r, dcol)
            spread(d_spread, True)

        @pl.when(jnp.logical_not(bottom))
        def _():
            make_link(dot(dcol[...], phi[...]), link_d, d_ref[...])
            for j in range(boxes):
                link_copy(link_d, in_d, ld_s, ld_r, after, j).start()

    @pl.when(final)
    def _():
        u_ref[...] = d_ref[...]

    @pl.when(jnp.logical_not(final))
    def _():
        u_copy.wait_recv()
        u_ref[...] = d_ref[...] + coupling * dot(up_buf[...], m_ref[...])

        @pl.when(jnp.logical_not(first))
        def _():
            send_u[...] = u_ref[...].astype(BF16)
            u_copy.start()

        @pl.loop(0, nblk)
        def _(j):
            res_copy(j).wait_recv()
            res[strip(j), :] = finite(
                phi[strip(j), :].astype(F32) + coupling * dot(res_in[strip(j), :], m_ref[...])
            )

            @pl.when(jnp.logical_not(first))
            def _():
                res_copy(j).start()

        @pl.when(jnp.logical_not(top))
        def _():
            d_spread(1).wait_recv()

    flat[...] = dot(dcol[...], res[...])

    @pl.when(first)
    def _():
        @pl.when(jnp.logical_not(bottom))
        def _():
            gather_cols(link_u, in_u, lu_s, lu_r, ucol)
            spread(u_spread, True)

        flat[...] += dot(ucol[...], psi[...])

        @pl.when(jnp.logical_not(top))
        def _():
            make_link(flat[...], link_u, u_ref[...])
            for j in range(boxes):
                link_copy(link_u, in_u, lu_s, lu_r, before, j).start()

    @pl.when(jnp.logical_not(first))
    def _():
        @pl.when(jnp.logical_not(bottom))
        def _():
            u_spread(1).wait_recv()

        flat[...] += dot(ucol[...], psi[...])

    for j in range(boxes):
        part3[j] = flat[pl.ds(2 * j, 2), :].astype(BF16)

    def last_copy(step):
        mate = lax.rem(box + step, boxes)
        return hop(part3.at[mate], last_in.at[step], f_s.at[step], f_r.at[step], me, mate)

    for step in range(1, boxes):
        last_copy(step).start()
    total = u_ref[...] + part3[box].astype(F32)
    for step in range(1, boxes):
        last_copy(step).wait_recv()
        total = total + last_in[step].astype(F32)
    out_ref[...] = total

    store_map.wait()
    for step in range(1, boxes):
        last_copy(step).wait_send()

    @pl.when(jnp.logical_not(final))
    def _():
        d_copy.wait_send()
        @pl.loop(0, nblk)
        def _(j):
            phi_copy(j).wait_send()

    @pl.when(jnp.logical_not(first))
    def _():
        u_copy.wait_send()
        @pl.loop(0, nblk)
        def _(j):
            psi_copy(j).wait_send()
            res_copy(j).wait_send()

    @pl.when(jnp.logical_and(final, jnp.logical_not(top)))
    def _():
        spread(d_spread, False)

    @pl.when(jnp.logical_and(final, jnp.logical_not(bottom)))
    def _():
        for j in range(boxes):
            link_copy(link_d, in_d, ld_s, ld_r, after, j).wait_send()

    @pl.when(jnp.logical_and(first, jnp.logical_not(bottom)))
    def _():
        spread(u_spread, False)

    @pl.when(jnp.logical_and(first, jnp.logical_not(top)))
    def _():
        for j in range(boxes):
            link_copy(link_u, in_u, lu_s, lu_r, before, j).wait_send()

    for k in range(width // CH):
        send(leaf, part0, k, s0, r0, sibling).wait_send()
    for base in ORDER:
        mine = base + core
        send(half1, part1, mine, s1, r1, pair).wait_send()
        send(half2, part2, mine, s2, r2, cross).wait_send()
        send(part1, part1, mine, q1, r1, sibling).wait_send()
        send(part2, part2, mine, q2, r2, sibling).wait_send()


def hand_on(m_in, u_in, m_out, u_out, m_buf, u_buf, sem):
    count = m_in.shape[0] // CH
    pairs = [(m_in, m_buf, m_out, pl.ds(k * CH, CH)) for k in range(count)]
    pairs.append((u_in, u_buf, u_out, pl.ds(0, u_in.shape[0])))
    loads, stores = [], []
    for k, (src, buf, dst, where) in enumerate(pairs):
        loads.append(pltpu.make_async_copy(src.at[where, :], buf.at[where, :], sem.at[2 * k]))
        stores.append(pltpu.make_async_copy(buf.at[where, :], dst.at[where, :], sem.at[2 * k + 1]))
    for load in loads:
        load.start()
    for load, store in zip(loads, stores):
        load.wait()
        store.start()
    for store in stores:
        store.wait()


def on_device(box_maps, block_pattern, face_inverses, index_map, sources):
    boxes = lax.axis_size("box")
    layers = lax.axis_size("layer")
    coupling = math.sqrt(boxes)
    width = box_maps.shape[2]
    rhs = sources.shape[1]
    face = face_inverses.shape[2]
    vmem = pl.BlockSpec(memory_space=pltpu.VMEM)
    anywhere = pl.BlockSpec(memory_space=pl.ANY)
    square = pltpu.VMEM((width, width), BF16)
    count = pltpu.SemaphoreType.DMA((width // CH,))
    merged, upward = pl.pallas_call(
        functools.partial(kernel, layers, coupling),
        out_shape=(
            jax.ShapeDtypeStruct((width, width), BF16),
            jax.ShapeDtypeStruct((rhs, width), F32),
        ),
        in_specs=[anywhere, pl.BlockSpec(memory_space=pltpu.SMEM), anywhere, vmem, vmem],
        out_specs=(anywhere, vmem),
        scratch_shapes=[
            square, square, pltpu.VMEM((3, face, face), F32), pltpu.SemaphoreType.DMA((16,)),
        ]
        + [square] * 6
        + [pltpu.VMEM((3, face, width), BF16), square, square]
        + [pltpu.VMEM((rhs, width), F32)] * 2
        + [pltpu.VMEM((rhs, width), BF16)] * 4
        + [pltpu.VMEM((CH, width), BF16)] * 6
        + [pltpu.VMEM((boxes * rhs, CH), BF16)] * 2
        + [pltpu.VMEM((boxes * rhs, width), F32)]
        + [pltpu.VMEM((boxes, rhs, width), BF16)]
        + [pltpu.VMEM((boxes * rhs, width), BF16)] * 2
        + [pltpu.VMEM((boxes, boxes * rhs, CH), BF16)] * 2
        + [pltpu.VMEM((boxes * rhs, width), F32), pltpu.VMEM((boxes, rhs, width), BF16)]
        + [count] * 8
        + [pltpu.SemaphoreType.DMA((8,))] * 6
        + [pltpu.SemaphoreType.DMA((2,))] * 2
        + [pltpu.SemaphoreType.DMA((boxes,))] * 8,
        compiler_params=pltpu.CompilerParams(
            collective_id=0, has_side_effects=True, vmem_limit_bytes=56 * 2**20
        ),
    )(box_maps[0], block_pattern[0], face_inverses[0], index_map, sources[0])
    merged, upward = pl.pallas_call(
        hand_on,
        out_shape=(
            jax.ShapeDtypeStruct((width, width), BF16),
            jax.ShapeDtypeStruct((rhs, width), F32),
        ),
        in_specs=[anywhere, anywhere],
        out_specs=(anywhere, anywhere),
        scratch_shapes=[
            square, pltpu.VMEM((rhs, width), F32), pltpu.SemaphoreType.DMA((18,)),
        ],
    )(merged, upward)
    return (merged[None], upward[None])


def solution(mesh):
    return jax.shard_map(
        on_device,
        mesh=mesh,
        in_specs=(
            P("layer", "box", None),
            P("layer", "box", None),
            P("layer", None, None, None),
            P("layer", None),
            P("layer", "box", None),
        ),
        out_specs=(P("layer", None, None), P("layer", "box", None)),
        check_vma=False,
    )
```
